512 devices in a mesh: dp: 16 (over x, y), expert: 32 (over z, core).
Axes of the slice: x: 4, y: 4, z: 16, core: 2. Of those that a mesh axis runs over, the one named last changes fastest.
Arguments:
- tokens: bfloat16 [65536, 2048], P(('dp', 'expert')), may hold values from -6 to 6
- cotangent: bfloat16 [65536, 2048], P(('dp', 'expert')), may hold values from -6 to 6
- routes: int32 [65536, 8], P(('dp', 'expert')), may hold values from 0 to 127, as said below
- slot_gates: float32 [65536, 8], P(('dp', 'expert')), may hold values from 0.05 to 0.5
- gate_up_weight: bfloat16 [32, 2, 2048, 768], P('expert', None, None, 'dp'), may hold values from -0.125 to 0.125
- down_master: float32 [32, 768, 2048], P('expert', 'dp'), may hold values from -0.21875 to 0.21875
- first_moment: float32 [32, 768, 2048], P('expert', 'dp'), may hold values from -4 to 4
- second_moment: float32 [32, 768, 2048], P('expert', 'dp'), may hold values from 0.5 to 4
Outputs:
- new_down: float32 [32, 768, 2048], P('expert', 'dp')
- new_first: float32 [32, 768, 2048], P('expert', 'dp')
- new_second: float32 [32, 768, 2048], P('expert', 'dp')
The draws below stay inside these ranges and needn't reach their ends.
Inputs may be any that keep to these rules, and one draw needn't show every extreme that they name: `routes`: each row names 8 different experts. In the 128 rows of one device no expert is named more than 24 times; in every group of devices that share a dp index, one expert below 32 is named exactly 24 times by every device of the group.
All inputs are finite; a program needn't handle non-finite values.
Results may differ from the reference program's by a relative error of at most 0.025.
Values may be sent and summed in bfloat16 or wider, within the bound.
A program may use at most 64 MiB of HBM per device.

```python
import math
import jax
import jax.numpy as jnp
from jax import lax

D = 2048
FF = 768
ROUTED = 128
TOPK = 8
TOK_DEV = 128
EXPERTS = 32
MOST = 24
TOKENS = 65536
N_DP = 16
N_EXPERT = 32


def draw_routes(key, part):
    blocks = TOKENS // TOK_DEV
    mean_load = TOK_DEV // 16
    position = jnp.arange(ROUTED, dtype=jnp.int32)
    base_counts = jnp.where(position < 8, 3 * mean_load, jnp.where(position < 32, 3 * mean_load // 2, jnp.where(position < 72, mean_load, mean_load // 2))).astype(jnp.int32)

    def one_block(block_index):
        block_key = jax.random.fold_in(key, block_index)
        group_index = block_index // EXPERTS
        hot_expert = jax.random.randint(jax.random.fold_in(jax.random.fold_in(key, 7919), group_index), (), 0, EXPERTS).astype(jnp.int32)
        expert_order = jax.random.permutation(jax.random.fold_in(block_key, 1), ROUTED).astype(jnp.int32)
        expert_order = jnp.where(expert_order == hot_expert, expert_order[0], expert_order).at[0].set(hot_expert)
        moved_rows = jax.random.randint(jax.random.fold_in(block_key, 2), (63,), 0, mean_load // 2 + 1).astype(jnp.int32)
        counts = base_counts.at[1:64].add(-moved_rows).at[65:128].add(moved_rows)
        count_ends = jnp.cumsum(counts)
        slot_index = jnp.arange(TOK_DEV * TOPK, dtype=jnp.int32)
        tier_index = jnp.sum((count_ends[None, :] <= slot_index[:, None]).astype(jnp.int32), axis=1)
        chosen = expert_order[tier_index].reshape(TOPK, TOK_DEV).T
        shuffle = jax.random.permutation(jax.random.fold_in(block_key, 3), TOK_DEV)
        return chosen[shuffle]
    return jax.vmap(one_block)(jnp.arange(blocks, dtype=jnp.int32)).reshape(TOKENS, TOPK).astype(jnp.int32)


def shard_levels(stream_key, dims, pieces, low, top_value):
    def one(dim, parts):
        heights = jax.random.uniform(jax.random.fold_in(jax.random.fold_in(stream_key, 6), dim), (parts,), jnp.float32, low / len(pieces), top_value / len(pieces))
        return jnp.repeat(jnp.exp(heights), dims[dim] // parts).reshape((-1,) + (1,) * (len(dims) - dim - 1))

    loudness = one(*pieces[0])
    for cut in pieces[1:]:
        loudness = loudness * one(*cut)
    return loudness


def noise(rng, shape, deviation, limit, shards=(), kind=jnp.bfloat16):
    result = deviation * jax.random.normal(rng, shape, jnp.float32)
    if shards:
        result = result * shard_levels(rng, shape, shards, -0.22, 0.18)
    return jnp.clip(result, -limit, limit).astype(kind)


def setup_inputs(seed: int = 0) -> dict:
    seeds = jax.random.split(jax.random.key(seed), 9)
    return {
        "tokens": noise(seeds[0], (TOKENS, D), 1.0, 6.0, ((0, 512),)),
        "cotangent": noise(seeds[1], (TOKENS, D), 1.0, 6.0, ((0, 512),)),
        "routes": draw_routes(jax.random.fold_in(seeds[8], 71), 0),
        "slot_gates": jnp.clip(jnp.exp(math.log(0.5) - 2.3025851 * jax.random.uniform(seeds[3], (TOKENS, TOPK), jnp.float32) ** shard_levels(seeds[3], (TOKENS, TOPK), ((0, 512),), -0.2, 0.2)), 0.05, 0.5),
        "gate_up_weight": noise(seeds[4], (EXPERTS, 2, D, FF), D ** -0.5, 0.125, ((0, 32), (3, 16))),
        "down_master": noise(seeds[5], (EXPERTS, FF, D), FF ** -0.5, 0.21875, ((0, 32), (1, 16)), jnp.float32),
        "first_moment": noise(seeds[6], (EXPERTS, FF, D), 0.5, 4.0, ((0, 32), (1, 16)), jnp.float32),
        "second_moment": jnp.clip(jnp.exp(math.log(4.0) - 2.0794415 * jax.random.uniform(seeds[7], (EXPERTS, FF, D), jnp.float32) ** shard_levels(seeds[7], (EXPERTS, FF, D), ((0, 32), (1, 16)), -0.2, 0.2)), 0.5, 4.0),
    }


BETA_ONE = 0.9
BETA_TWO = 0.95
LEARN_RATE = 0.003
DECAY_RATE = 0.1
ADAM_EPS = 1e-08

def pack_rows(features, cotangent, routes, slot_gates, experts, most):
    tok_rows = routes.shape[0]
    top_count = routes.shape[1]
    flat_routes = routes.reshape(-1)
    flat_gates = slot_gates.reshape(-1)
    expert_ids = jnp.arange(experts, dtype=jnp.int32)
    one_hot = (flat_routes[:, None] == expert_ids[None, :]).astype(jnp.int32)
    earlier = jnp.cumsum(one_hot, axis=0) - one_hot
    slot_rank = lax.optimization_barrier(jnp.sum(earlier * one_hot, axis=1))
    in_window = flat_routes < experts
    slot_place = jnp.where(in_window, flat_routes * most + slot_rank, experts * most).astype(jnp.int32)
    slot_owner = (jnp.arange(tok_rows * top_count, dtype=jnp.int32) // top_count).astype(jnp.int32)
    slot_token = jnp.zeros((experts * most,), jnp.int32).at[slot_place].set(slot_owner, mode='drop')
    slot_weight = jnp.zeros((experts * most,), flat_gates.dtype).at[slot_place].set(flat_gates, mode='drop')
    slot_filled = jnp.zeros((experts * most,), jnp.int32).at[slot_place].set(1, mode='drop')
    picked = features[slot_token]
    rows_x = jnp.where(slot_filled[:, None] > 0, picked, jnp.zeros_like(picked))
    rows_c = (cotangent[slot_token].astype(jnp.float32) * slot_weight[:, None]).astype(jnp.bfloat16)
    model_width = features.shape[1]
    return (rows_x.reshape(experts, most, model_width), rows_c.reshape(experts, most, model_width))

def reference(tokens, cotangent, routes, slot_gates, gate_up_weight, down_master, first_moment, second_moment):
    group_rows = N_EXPERT * TOK_DEV

    def one_group(group_index):
        row_start = group_index * group_rows
        feats = lax.dynamic_slice_in_dim(tokens, row_start, group_rows, 0).reshape(N_EXPERT, TOK_DEV, D)
        cotan = lax.dynamic_slice_in_dim(cotangent, row_start, group_rows, 0).reshape(N_EXPERT, TOK_DEV, D)
        chosen = lax.dynamic_slice_in_dim(routes, row_start, group_rows, 0).reshape(N_EXPERT, TOK_DEV, TOPK)
        weights = lax.dynamic_slice_in_dim(slot_gates, row_start, group_rows, 0).reshape(N_EXPERT, TOK_DEV, TOPK)
        rows_x, rows_c = jax.vmap(lambda fa, fb, fc, fd: pack_rows(fa, fb, fc, fd, EXPERTS, MOST))(feats, cotan, chosen, weights)

        def one_expert(expert_index):
            recv_x = jnp.take(rows_x, expert_index, axis=1).reshape(-1, D)
            recv_c = jnp.take(rows_c, expert_index, axis=1).reshape(-1, D)
            expert_weight = jnp.take(gate_up_weight, expert_index, axis=0)
            gate_part = jnp.dot(recv_x, expert_weight[0], preferred_element_type=jnp.float32)
            up_part = jnp.dot(recv_x, expert_weight[1], preferred_element_type=jnp.float32)
            hidden = (jax.nn.silu(gate_part) * up_part).astype(jnp.bfloat16)
            partial_grad = jnp.dot(hidden.T, recv_c, preferred_element_type=jnp.float32)
            return partial_grad.astype(jnp.bfloat16)
        return lax.map(one_expert, jnp.arange(EXPERTS, dtype=jnp.int32))

    def add_group(running, group_index):
        return (running + one_group(group_index).astype(jnp.float32), None)
    grad, _ = lax.scan(add_group, jnp.zeros((EXPERTS, FF, D), jnp.float32), jnp.arange(N_DP, dtype=jnp.int32))
    new_first = BETA_ONE * first_moment + (1.0 - BETA_ONE) * grad
    new_second = BETA_TWO * second_moment + (1.0 - BETA_TWO) * grad * grad
    new_down = down_master - LEARN_RATE * (new_first / (jnp.sqrt(new_second) + ADAM_EPS) + DECAY_RATE * down_master)
    return (new_down, new_first, new_second)
```

```python
import functools

import jax
import jax.numpy as jnp
from jax import lax
from jax.experimental import pallas as pl
from jax.experimental.pallas import tpu as pltpu
from jax.sharding import PartitionSpec as P

MOST = 24
NQ = 4
OFFSETS = (0, 0, 1, 1)

BETA_ONE = 0.9
BETA_TWO = 0.95
LEARN_RATE = 0.003
DECAY_RATE = 0.1
ADAM_EPS = 1e-08

MESH = pl.DeviceIdType.MESH
F32 = jnp.float32
BF16 = jnp.bfloat16


def kernel(
    ndp, ne,
    x_ref, c_ref, rt_ref, gt_ref, w_ref,
    grad_ref,
    buf, w_all, g_all, p_all, gate_all, rows, ht, ps, land,
    loc_sem, rr, rs, pr, psd, wr, ws, lr_sem, ls_sem,
):
    nz = ne // 2
    items = 2 * NQ
    hops = nz // 2 + 1
    toks = buf.shape[2]
    cw = buf.shape[3]
    width = NQ * cw
    pair = 2 * MOST
    nrows = nz * pair
    fd = w_ref.shape[1]
    ff = ndp * fd

    me = lax.axis_index("expert")
    dp = lax.axis_index("dp")
    z = me // 2
    core = me % 2
    partner = me + 1 - 2 * core

    def zslot(d):
        return 2 * ((z + d + nz) % nz) + core

    def load(k, t, q):
        src = x_ref if t == 0 else c_ref
        return pltpu.make_async_copy(
            src.at[:, pl.ds(q * cw, cw)], buf.at[k, me], loc_sem.at[k]
        )

    for q in range(NQ):
        load(q, 0, q).start()
    for q in range(NQ):
        load(NQ + q, 1, q).start()
    w_load = pltpu.make_async_copy(w_ref, w_all.at[:, dp], loc_sem.at[items])
    w_load.start()

    expert_id = lax.broadcasted_iota(jnp.int32, (ne, toks), 0)
    table = jnp.zeros((ne, toks), F32)
    for k in range(rt_ref.shape[0]):
        table = table + jnp.where(rt_ref[k : k + 1, :] == expert_id, gt_ref[k : k + 1, :], 0.0)
    g_all[me] = table

    barrier = pltpu.get_barrier_semaphore()
    for other in (zslot(1), zslot(-1), partner):
        pl.semaphore_signal(barrier, inc=1, device_id={"expert": other}, device_id_type=MESH)

    @pl.loop(1, ndp)
    def _(d):
        pl.semaphore_signal(
            barrier, inc=1, device_id={"dp": (dp + d) % ndp}, device_id_type=MESH
        )

    pl.semaphore_wait(barrier, 3 + ndp - 1)

    def chunk(k, s):
        return g_all.at[s] if k is None else buf.at[k, s]

    def sidx(k):
        return items if k is None else k

    def ring_copy(k, direction, s, h):
        return pltpu.make_async_remote_copy(
            src_ref=chunk(k, s), dst_ref=chunk(k, s),
            send_sem=rs.at[sidx(k), direction, h],
            recv_sem=rr.at[sidx(k), direction, h + 1],
            device_id={"expert": zslot(1 if direction == 0 else -1)},
            device_id_type=MESH,
        )

    def ring_arrived(k, direction, s, h):
        pltpu.make_async_remote_copy(
            src_ref=chunk(k, s), dst_ref=chunk(k, s),
            send_sem=rs.at[sidx(k), direction, h],
            recv_sem=rr.at[sidx(k), direction, h],
            device_id={"expert": zslot(1 if direction == 0 else -1)},
            device_id_type=MESH,
        ).wait_recv()

    def partner_copy(k, s, zz):
        return pltpu.make_async_remote_copy(
            src_ref=chunk(k, s), dst_ref=chunk(k, s),
            send_sem=psd.at[sidx(k), zz], recv_sem=pr.at[sidx(k), zz],
            device_id={"expert": partner}, device_id_type=MESH,
        )

    def reach(parity, direction):
        return nz // 2 if parity == direction else nz // 2 - 1

    def event(k, parity, h, ready):
        @pl.when(h == 0)
        def _():
            ready()
            ring_copy(k, 0, me, 0).start()
            ring_copy(k, 1, me, 0).start()
            partner_copy(k, me, z).start()

        for direction in range(2):
            last = reach(parity, direction)

            @pl.when((h > 0) & (h <= last))
            def _():
                d = -h if direction == 0 else h
                s = zslot(d)
                ring_arrived(k, direction, s, h)

                @pl.when(h < last)
                def _():
                    ring_copy(k, direction, s, h).start()

                partner_copy(k, s, s // 2).start()

    def pairs(k, parity, h, work):
        def one(zz):
            partner_copy(k, 2 * zz + 1 - core, zz).wait_recv()
            work(zz)

        @pl.when(h == 0)
        def _():
            one(z)

        for direction in range(2):
            @pl.when((h > 0) & (h <= reach(parity, direction)))
            def _():
                one(zslot(-h if direction == 0 else h) // 2)

    def build(zz):
        both = jnp.concatenate(
            [g_all[2 * zz, pl.ds(me, 1), :], g_all[2 * zz + 1, pl.ds(me, 1), :]], axis=0
        )
        mask = jnp.where(both > 0.0, 1.0, 0.0)
        row_id = lax.broadcasted_iota(jnp.int32, (toks, toks), 0)
        col_id = lax.broadcasted_iota(jnp.int32, (toks, toks), 1)
        before = jnp.where(row_id < col_id, 1.0, 0.0).astype(BF16)
        padded = jnp.concatenate([mask, jnp.zeros((6, toks), F32)], axis=0)
        rank = jnp.dot(padded.astype(BF16), before, preferred_element_type=F32)
        places = []
        for s in range(2):
            places.append(
                jnp.where(mask[s : s + 1, :] > 0.0, rank[s : s + 1, :] + float(MOST * s), -1.0)
            )
        place = jnp.concatenate(places, axis=1)
        gates = jnp.concatenate([both[0:1, :], both[1:2, :]], axis=1)
        wanted = lax.broadcasted_iota(jnp.int32, (pair, 2 * toks), 0).astype(F32)
        hit = wanted == place
        p_all[zz] = jnp.where(hit, 1.0, 0.0).astype(BF16)
        gate = jnp.sum(jnp.where(hit, gates, 0.0), axis=1, keepdims=True)
        gate_all[zz] = jnp.broadcast_to(gate, (pair, 128))

    def select(k, zz):
        both = buf[k, pl.ds(2 * zz, 2)].reshape(2 * toks, cw)
        got = jnp.dot(p_all[zz], both, preferred_element_type=F32)
        gate = gate_all[zz][:, 0:1]
        scale = jnp.where(k >= NQ, gate, jnp.ones_like(gate))
        rows[k, pl.ds(pl.multiple_of(zz * pair, 16), pair), :] = (got * scale).astype(BF16)

    fsplit = 2
    fb = ff // fsplit
    rb = 256 if nrows % 256 == 0 else nrows
    rsplit = nrows // rb
    pieces = fsplit * rsplit

    def nt(a, b):
        return lax.dot_general(a, b, (((1,), (1,)), ((), ())), preferred_element_type=F32)

    def hidden_piece(p):
        f0 = p // rsplit
        r0 = p % rsplit
        gate = jnp.zeros((fb, rb), F32)
        up = jnp.zeros((fb, rb), F32)
        for q in range(NQ):
            xs = rows[q, pl.ds(pl.multiple_of(r0 * rb, 16), rb), :]
            blocks = pl.ds(f0 * (ndp // fsplit), ndp // fsplit)
            cols = pl.ds(q * cw, cw)
            gate = gate + nt(w_all[0, blocks, :, cols].reshape(fb, cw), xs)
            up = up + nt(w_all[1, blocks, :, cols].reshape(fb, cw), xs)
        act = gate / (1.0 + jnp.exp(-gate)) * up
        ht[pl.ds(pl.multiple_of(f0 * fb, 16), fb), pl.ds(pl.multiple_of(r0 * rb, 128), rb)] = act.astype(BF16)

    def w_copy(other, slot):
        return pltpu.make_async_remote_copy(
            src_ref=w_all.at[:, slot], dst_ref=w_all.at[:, slot],
            send_sem=ws.at[other], recv_sem=wr.at[slot],
            device_id={"dp": other}, device_id_type=MESH,
        )

    def r_copy(q, other, slot):
        return pltpu.make_async_remote_copy(
            src_ref=ps.at[q, other], dst_ref=land.at[q, slot],
            send_sem=ls_sem.at[q, other], recv_sem=lr_sem.at[q, slot],
            device_id={"dp": other}, device_id_type=MESH,
        )

    def partial(q):
        for f0 in range(fsplit):
            part = jnp.dot(
                ht[f0 * fb : (f0 + 1) * fb, :], rows[NQ + q], preferred_element_type=F32
            )
            per = ndp // fsplit
            ps[q, f0 * per : (f0 + 1) * per] = part.astype(BF16).reshape(per, fd, cw)
        land[q, dp] = ps[q, dp]

        @pl.loop(1, ndp)
        def _(d):
            r_copy(q, (dp + d) % ndp, dp).start()

    x_done = max(OFFSETS) + hops

    @pl.loop(0, 2 * hops + max(OFFSETS) + 1)
    def _(r):
        @pl.when(r < hops)
        def _():
            event(None, 0, r, lambda: None)

        for j in range(NQ):
            lr = r - OFFSETS[j]

            @pl.when((lr >= 0) & (lr < 2 * hops))
            def _():
                second = lr // hops
                k = j + NQ * second
                event(k, j % 2, lr % hops, lambda: load(k, 0, j).wait())

        @pl.when(r == 0)
        def _():
            w_load.wait()

            @pl.loop(1, ndp)
            def _(d):
                w_copy((dp + d) % ndp, dp).start()

        @pl.when(r == x_done + 1)
        def _():
            @pl.loop(1, ndp)
            def _(d):
                other = (dp + d) % ndp
                w_copy(other, other).wait_recv()

        @pl.when((r > x_done) & (r <= x_done + pieces))
        def _():
            hidden_piece(r - x_done - 1)

        @pl.when((r >= 1) & (r <= hops))
        def _():
            pairs(None, 0, r - 1, build)

        for j in range(NQ):
            late = r - 1 - OFFSETS[j]

            @pl.when((late >= 0) & (late < 2 * hops))
            def _():
                k = j + NQ * (late // hops)
                pairs(k, j % 2, late % hops, functools.partial(select, k))

            @pl.when(late == 2 * hops - 1)
            def _():
                partial(j)

    for q in range(NQ):
        @pl.loop(1, ndp)
        def _(d):
            other = (dp + d) % ndp
            r_copy(q, other, other).wait_recv()

        total = land[q, 0].astype(F32)
        for i in range(1, ndp):
            total = total + land[q, i].astype(F32)
        grad_ref[:, q * cw : (q + 1) * cw] = total

    def drain(k, parity):
        for direction in range(2):
            @pl.loop(0, reach(parity, direction))
            def _(h):
                ring_copy(k, direction, me, h).wait_send()

        @pl.loop(0, nz)
        def _(zz):
            partner_copy(k, me, zz).wait_send()

    drain(None, 0)

    @pl.loop(0, items // 2)
    def _(half):
        for parity in range(2):
            drain(2 * half + parity, parity)

    @pl.loop(1, ndp)
    def _(d):
        other = (dp + d) % ndp
        w_copy(other, dp).wait_send()
        for q in range(NQ):
            r_copy(q, other, dp).wait_send()


def grad_kernel(mesh, tokens, cotangent, routes_t, gates_t, weight):
    ndp = mesh.shape["dp"]
    ne = mesh.shape["expert"]
    nz = ne // 2
    toks, width = tokens.shape
    cw = width // NQ
    fd = weight.shape[1]
    items = 2 * NQ
    hops = nz // 2 + 1
    nrows = ne * MOST
    dma = pltpu.SemaphoreType.DMA
    anywhere = pl.BlockSpec(memory_space=pl.ANY)
    vmem = pl.BlockSpec(memory_space=pltpu.VMEM)
    return pl.pallas_call(
        functools.partial(kernel, ndp, ne),
        out_shape=jax.ShapeDtypeStruct((fd, width), F32),
        in_specs=[anywhere, anywhere, vmem, vmem, anywhere],
        out_specs=vmem,
        scratch_shapes=[
            pltpu.VMEM((items, ne, toks, cw), BF16),
            pltpu.VMEM((2, ndp, fd, width), BF16),
            pltpu.VMEM((ne, ne, toks), F32),
            pltpu.VMEM((nz, 2 * MOST, 2 * toks), BF16),
            pltpu.VMEM((nz, 2 * MOST, 128), F32),
            pltpu.VMEM((items, nrows, cw), BF16),
            pltpu.VMEM((ndp * fd, nrows), BF16),
            pltpu.VMEM((NQ, ndp, fd, cw), BF16),
            pltpu.VMEM((NQ, ndp, fd, cw), BF16),
            dma((items + 1,)),
            dma((items + 1, 2, hops)),
            dma((items + 1, 2, hops)),
            dma((items + 1, nz)),
            dma((items + 1, nz)),
            dma((ndp,)),
            dma((ndp,)),
            dma((NQ, ndp)),
            dma((NQ, ndp)),
        ],
        compiler_params=pltpu.CompilerParams(
            collective_id=0, has_side_effects=True, vmem_limit_bytes=67043328
        ),
        name="expert_grad",
    )(tokens, cotangent, routes_t, gates_t, weight)


def solution(mesh):
    def per_device(
        tokens, cotangent, routes, slot_gates, gate_up_weight, down_master, first_moment, second_moment
    ):
        grad = grad_kernel(
            mesh, tokens, cotangent, routes.T, slot_gates.T, jnp.swapaxes(gate_up_weight[0], 1, 2)
        )
        master = down_master[0]
        new_first = BETA_ONE * first_moment[0] + (1.0 - BETA_ONE) * grad
        new_second = BETA_TWO * second_moment[0] + (1.0 - BETA_TWO) * grad * grad
        new_down = master - LEARN_RATE * (
            new_first / (jnp.sqrt(new_second) + ADAM_EPS) + DECAY_RATE * master
        )
        return (new_down[None], new_first[None], new_second[None])

    return jax.shard_map(
        per_device,
        mesh=mesh,
        in_specs=(
            P(("dp", "expert"), None),
            P(("dp", "expert"), None),
            P(("dp", "expert"), None),
            P(("dp", "expert"), None),
            P("expert", None, None, "dp"),
            P("expert", "dp", None),
            P("expert", "dp", None),
            P("expert", "dp", None),
        ),
        out_specs=(P("expert", "dp", None), P("expert", "dp", None), P("expert", "dp", None)),
        check_vma=False,
    )
```

```python
import functools

import jax
import jax.numpy as jnp
from jax import lax
from jax.experimental import pallas as pl
from jax.experimental.pallas import tpu as pltpu
from jax.sharding import PartitionSpec as P

MOST = 24
NQ = 4
C_START = (0, 1, 3, 5)
SIDE = 4
PEER_ORDER = (
    (0, 1), (1, 0), (0, -1), (-1, 0), (1, 1), (-1, -1), (1, -1), (-1, 1),
    (0, 2), (2, 0), (1, 2), (2, 1), (-1, 2), (2, -1), (2, 2),
)

BETA_ONE = 0.9
BETA_TWO = 0.95
LEARN_RATE = 0.003
DECAY_RATE = 0.1
ADAM_EPS = 1e-08

MESH = pl.DeviceIdType.MESH
F32 = jnp.float32
BF16 = jnp.bfloat16


def kernel(
    ndp, ne,
    x_ref, c_ref, rt_ref, gt_ref, w_ref,
    grad_ref,
    buf, w_all, g_all, p_all, gate_all, rows, ht, ps, land, pm, po, pin,
    loc_sem, rr, rs, pr, psd, wr, ws, lr_sem, ls_sem, pos, pfs, pps,
):
    nz = ne // 2
    items = 2 * NQ
    hops = nz // 2 + 1
    toks = buf.shape[2]
    cw = buf.shape[3]
    width = NQ * cw
    pair = 2 * MOST
    nrows = nz * pair
    fd = w_ref.shape[1]
    ff = ndp * fd
    side = SIDE

    me = lax.axis_index("expert")
    dp = lax.axis_index("dp")
    z = me // 2
    core = me % 2
    partner = me + 1 - 2 * core

    def zslot(d):
        return 2 * ((z + d + nz) % nz) + core

    def load(k, t, q):
        src = x_ref if t == 0 else c_ref
        return pltpu.make_async_copy(
            src.at[:, pl.ds(q * cw, cw)], buf.at[k, me], loc_sem.at[k]
        )

    for q in range(NQ):
        load(q, 0, q).start()
    for q in range(NQ):
        load(NQ + q, 1, q).start()
    w_load = pltpu.make_async_copy(w_ref, w_all.at[:, dp], loc_sem.at[items])
    w_load.start()

    expert_id = lax.broadcasted_iota(jnp.int32, (ne, toks), 0)
    table = jnp.zeros((ne, toks), F32)
    for k in range(rt_ref.shape[0]):
        table = table + jnp.where(rt_ref[k : k + 1, :] == expert_id, gt_ref[k : k + 1, :], 0.0)
    g_all[me] = table

    barrier = pltpu.get_barrier_semaphore()
    for other in (zslot(1), zslot(-1), partner):
        pl.semaphore_signal(barrier, inc=1, device_id={"expert": other}, device_id_type=MESH)

    @pl.loop(1, ndp)
    def _(d):
        pl.semaphore_signal(
            barrier, inc=1, device_id={"dp": (dp + d) % ndp}, device_id_type=MESH
        )

    pl.semaphore_wait(barrier, 3 + ndp - 1)

    def chunk(k, s):
        return g_all.at[s] if k is None else buf.at[k, s]

    def sidx(k):
        return items if k is None else k

    def ring_copy(k, direction, s, h):
        return pltpu.make_async_remote_copy(
            src_ref=chunk(k, s), dst_ref=chunk(k, s),
            send_sem=rs.at[sidx(k), direction],
            recv_sem=rr.at[sidx(k), direction, h + 1],
            device_id={"expert": zslot(1 if direction == 0 else -1)},
            device_id_type=MESH,
        )

    def ring_arrived(k, direction, s, h):
        pltpu.make_async_remote_copy(
            src_ref=chunk(k, s), dst_ref=chunk(k, s),
            send_sem=rs.at[sidx(k), direction],
            recv_sem=rr.at[sidx(k), direction, h],
            device_id={"expert": zslot(1 if direction == 0 else -1)},
            device_id_type=MESH,
        ).wait_recv()

    def partner_copy(k, s, zz):
        return pltpu.make_async_remote_copy(
            src_ref=chunk(k, s), dst_ref=chunk(k, s),
            send_sem=psd.at[sidx(k)], recv_sem=pr.at[sidx(k), zz],
            device_id={"expert": partner}, device_id_type=MESH,
        )

    def reach(parity, direction):
        return nz // 2 if parity == direction else nz // 2 - 1

    def full_reach(k, parity, direction):
        return reach(parity, direction) - (0 if k is None else 2)

    def packed_copy(k, direction, src, dst, sem, h):
        return pltpu.make_async_remote_copy(
            src_ref=src, dst_ref=dst, send_sem=sem.at[k, direction],
            recv_sem=rr.at[k, direction, h],
            device_id={"expert": zslot(1 if direction == 0 else -1)},
            device_id_type=MESH,
        )

    def packed_first(k, parity, direction):
        return packed_copy(
            k, direction, po.at[k, direction], pin.at[k, direction, pl.ds(0, 2), core],
            pos, reach(parity, direction) - 1,
        )

    def packed_second(k, parity, direction):
        return packed_copy(
            k, direction, pin.at[k, direction, 1, core], pin.at[k, direction, 2, core],
            pfs, reach(parity, direction),
        )

    def packed_partner(k, direction, slot, zz, side_core):
        ref = pin.at[k, direction, slot, side_core]
        return pltpu.make_async_remote_copy(
            src_ref=ref, dst_ref=ref, send_sem=pps.at[k], recv_sem=pr.at[k, zz],
            device_id={"expert": partner}, device_id_type=MESH,
        )

    def event(k, parity, h, ready):
        @pl.when(h == 0)
        def _():
            ready()
            ring_copy(k, 0, me, 0).start()
            ring_copy(k, 1, me, 0).start()
            partner_copy(k, me, z).start()

        for direction in range(2):
            last = full_reach(k, parity, direction)
            s = zslot(-h if direction == 0 else h)

            @pl.when((h > 0) & (h <= last))
            def _():
                ring_arrived(k, direction, s, h)

                @pl.when(h < last)
                def _():
                    ring_copy(k, direction, s, h).start()

                partner_copy(k, s, s // 2).start()

            if k is not None:
                @pl.when(h == last)
                def _():
                    few = jnp.dot(
                        pm[direction, int(parity == direction)], buf[k, s],
                        preferred_element_type=F32,
                    )
                    po[k, direction] = few.astype(BF16).reshape(2, pair, cw)

                @pl.when(h == last + 1)
                def _():
                    packed_first(k, parity, direction).wait_recv()
                    packed_second(k, parity, direction).start()
                    packed_partner(k, direction, 0, s // 2, core).start()

                @pl.when(h == last + 2)
                def _():
                    packed_second(k, parity, direction).wait_recv()
                    packed_partner(k, direction, 2, s // 2, core).start()

    def send_packed(k, parity, h):
        for direction in range(2):
            @pl.when(h == full_reach(k, parity, direction))
            def _():
                packed_first(k, parity, direction).start()

    def pairs(k, parity, h, work, packed_work):
        def one(zz):
            partner_copy(k, 2 * zz + 1 - core, zz).wait_recv()
            work(zz)

        @pl.when(h == 0)
        def _():
            one(z)

        for direction in range(2):
            last = full_reach(k, parity, direction)
            zz = zslot(-h if direction == 0 else h) // 2

            @pl.when((h > 0) & (h <= last))
            def _():
                one(zz)

            if k is not None:
                for slot in (0, 2):
                    @pl.when(h == last + 1 + slot // 2)
                    def _():
                        packed_partner(k, direction, slot, zz, 1 - core).wait_recv()
                        packed_work(zz, direction, slot)

    def ranks(mask):
        row_id = lax.broadcasted_iota(jnp.int32, (toks, toks), 0)
        col_id = lax.broadcasted_iota(jnp.int32, (toks, toks), 1)
        before = jnp.where(row_id < col_id, 1.0, 0.0).astype(BF16)
        padded = jnp.concatenate([mask, jnp.zeros((8 - mask.shape[0], toks), F32)], axis=0)
        return jnp.dot(padded.astype(BF16), before, preferred_element_type=F32)

    def build_pack(direction, long, s):
        parts = []
        for ahead in (1, 2):
            dest = zslot(ahead if direction == 0 else -ahead) // 2
            for other in range(2):
                parts.append(g_all[s, pl.ds(2 * dest + other, 1), :])
        mask = jnp.where(jnp.concatenate(parts, axis=0) > 0.0, 1.0, 0.0)
        rank = ranks(mask)
        wanted = lax.broadcasted_iota(jnp.int32, (2 * pair, toks), 0).astype(F32)
        total = jnp.zeros((2 * pair, toks), F32)
        for i in range(4):
            place = jnp.where(mask[i : i + 1, :] > 0.0, rank[i : i + 1, :] + float(MOST * i), -1.0)
            total = total + jnp.where(wanted == place, 1.0, 0.0)
        pm[direction, long] = total.astype(BF16)

    def build(zz):
        both = jnp.concatenate(
            [g_all[2 * zz, pl.ds(me, 1), :], g_all[2 * zz + 1, pl.ds(me, 1), :]], axis=0
        )
        mask = jnp.where(both > 0.0, 1.0, 0.0)
        rank = ranks(mask)
        places = []
        for s in range(2):
            places.append(
                jnp.where(mask[s : s + 1, :] > 0.0, rank[s : s + 1, :] + float(MOST * s), -1.0)
            )
        place = jnp.concatenate(places, axis=1)
        gates = jnp.concatenate([both[0:1, :], both[1:2, :]], axis=1)
        wanted = lax.broadcasted_iota(jnp.int32, (pair, 2 * toks), 0).astype(F32)
        hit = wanted == place
        p_all[zz] = jnp.where(hit, 1.0, 0.0).astype(BF16)
        gate = jnp.sum(jnp.where(hit, gates, 0.0), axis=1, keepdims=True)
        gate_all[zz] = jnp.broadcast_to(gate, (pair, 128))

    def keep(k, zz, got):
        gate = gate_all[zz][:, 0:1]
        scale = jnp.where(k >= NQ, gate, jnp.ones_like(gate))
        rows[k, pl.ds(pl.multiple_of(zz * pair, 16), pair), :] = (got * scale).astype(BF16)

    def select(k, zz):
        both = buf[k, pl.ds(2 * zz, 2)].reshape(2 * toks, cw)
        keep(k, zz, jnp.dot(p_all[zz], both, preferred_element_type=F32))

    def select_packed(k, zz, direction, slot):
        both = pin[k, direction, slot].reshape(2 * pair, cw)
        to = lax.broadcasted_iota(jnp.int32, (pair, 2 * pair), 0)
        of = lax.broadcasted_iota(jnp.int32, (pair, 2 * pair), 1)
        mine = to + MOST * core + jnp.where(to >= MOST, MOST, 0)
        pick = jnp.where(of == mine, 1.0, 0.0).astype(BF16)
        keep(k, zz, jnp.dot(pick, both, preferred_element_type=F32))

    fsplit = 2
    fb = ff // fsplit
    rb = 256 if nrows % 256 == 0 else nrows
    rsplit = nrows // rb
    pieces = fsplit * rsplit

    def nt(a, b):
        return lax.dot_general(a, b, (((1,), (1,)), ((), ())), preferred_element_type=F32)

    def hidden_piece(p):
        f0 = p // rsplit
        r0 = p % rsplit
        gate = jnp.zeros((fb, rb), F32)
        up = jnp.zeros((fb, rb), F32)
        for q in range(NQ):
            xs = rows[q, pl.ds(pl.multiple_of(r0 * rb, 16), rb), :]
            blocks = pl.ds(f0 * (ndp // fsplit), ndp // fsplit)
            cols = pl.ds(q * cw, cw)
            gate = gate + nt(w_all[0, blocks, :, cols].reshape(fb, cw), xs)
            up = up + nt(w_all[1, blocks, :, cols].reshape(fb, cw), xs)
        act = gate / (1.0 + jnp.exp(-gate)) * up
        ht[pl.ds(pl.multiple_of(f0 * fb, 16), fb), pl.ds(pl.multiple_of(r0 * rb, 128), rb)] = act.astype(BF16)

    def offset_peer(u, v):
        return ((dp // side + u + side) % side) * side + (dp % side + v + side) % side

    def w_copy(p, slot, half, u, v):
        ref = w_all.at[p, slot]
        if half is not None:
            ref = w_all.at[p, slot, :, pl.ds(half * (width // 2), width // 2)]
        return pltpu.make_async_remote_copy(
            src_ref=ref, dst_ref=ref, send_sem=ws, recv_sem=wr.at[p, slot, half or 0],
            device_id={"dp": offset_peer(u, v)}, device_id_type=MESH,
        )

    def w_hop(p, axis, slot, half, step):
        along_x = (p == 0) == (axis == 0)
        return w_copy(p, slot, half, step if along_x else 0, 0 if along_x else step)

    def w_slot(p, u, v):
        return offset_peer(u, v) if p == 0 else offset_peer(v, u)

    def w_step(n):
        for p in range(2):
            if n == 0:
                for axis in range(2):
                    for step in (1, -1):
                        w_hop(p, axis, dp, None, step).start()
                continue
            if n == 1:
                for step in (1, -1):
                    slot = w_slot(p, -step, 0)
                    w_hop(p, 0, slot, None, step).wait_recv()
                    w_hop(p, 0, slot, 0 if step == 1 else 1, step).start()
                    for step2 in (1, -1):
                        w_hop(p, 1, slot, None, step2).start()
            if n == 2:
                slot = w_slot(p, 2, 0)
                for half in range(2):
                    w_hop(p, 0, slot, half, 1).wait_recv()
                for step2 in (1, -1):
                    w_hop(p, 1, slot, None, step2).start()
            for u in ((0,), (1, -1), (2,))[n - 1] if n < 4 else ():
                for step in (1, -1):
                    slot = w_slot(p, u, -step)
                    w_hop(p, 1, slot, None, step).wait_recv()
                    w_hop(p, 1, slot, 0 if step == 1 else 1, step).start()
            if n == 4:
                for u in (0, 1, -1, 2):
                    for half in range(2):
                        w_hop(p, 1, w_slot(p, u, 2), half, 1).wait_recv()

    def w_sent():
        ref = w_all.at[:, pl.ds(0, ndp - 1)]
        pltpu.make_async_remote_copy(
            src_ref=ref, dst_ref=ref, send_sem=ws, recv_sem=wr.at[0, 0, 0],
            device_id={"dp": offset_peer(1, 0)}, device_id_type=MESH,
        ).wait_send()

    def r_copy(q, other):
        return pltpu.make_async_remote_copy(
            src_ref=ps.at[q, other], dst_ref=land.at[q, dp],
            send_sem=ls_sem.at[q], recv_sem=lr_sem.at[q],
            device_id={"dp": other}, device_id_type=MESH,
        )

    def r_all(q):
        return pltpu.make_async_remote_copy(
            src_ref=ps.at[q, pl.ds(0, ndp - 1)], dst_ref=land.at[q, pl.ds(0, ndp - 1)],
            send_sem=ls_sem.at[q], recv_sem=lr_sem.at[q],
            device_id={"dp": offset_peer(1, 0)}, device_id_type=MESH,
        )

    def partial(q):
        for f0 in range(fsplit):
            part = jnp.dot(
                ht[f0 * fb : (f0 + 1) * fb, :], rows[NQ + q], preferred_element_type=F32
            )
            per = ndp // fsplit
            ps[q, f0 * per : (f0 + 1) * per] = part.astype(BF16).reshape(per, fd, cw)
        land[q, dp] = ps[q, dp]

        for u, v in PEER_ORDER:
            r_copy(q, offset_peer(u, v)).start()

    def lane(j, r, work):
        period = hops + C_START[j]
        h = r % period

        @pl.when((r >= 0) & (r < 2 * period) & (h < hops))
        def _():
            work(j + NQ * (r // period), h)

    def compute(j, r):
        def work(k, h):
            pairs(k, j % 2, h, functools.partial(select, k), functools.partial(select_packed, k))

        lane(j, r, work)

        @pl.when(r == 2 * hops + C_START[j] - 1)
        def _():
            partial(j)

    @pl.loop(0, 2 * hops + max(C_START) + 1)
    def _(r):
        @pl.when(r < hops)
        def _():
            event(None, 0, r, lambda: None)

        for direction in range(2):
            for long in range(2):
                h = nz // 2 - 3 + long

                @pl.when(r == h)
                def _():
                    build_pack(direction, long, zslot(-h if direction == 0 else h))

        for j in range(NQ):
            lane(j, r, lambda k, h: event(k, j % 2, h, lambda: load(k, 0, j).wait()))
            compute((j + 2) % NQ, r if j >= 2 else r - 1)
            lane(j, r, lambda k, h: send_packed(k, j % 2, h))

            if j == 1:
                @pl.when(r < hops)
                def _():
                    pairs(None, 0, r, build, None)

        for n in range(4):
            @pl.when(r == n)
            def _():
                if n == 0:
                    w_load.wait()
                w_step(n)

        @pl.when(r == hops + 1)
        def _():
            w_step(4)

        @pl.when((r > hops) & (r <= hops + pieces))
        def _():
            hidden_piece(r - hops - 1)

    def ring_sent(k, parity):
        for direction in range(2):
            count = pl.ds(0, full_reach(k, parity, direction))
            ref = g_all.at[count] if k is None else buf.at[k, count]
            pltpu.make_async_remote_copy(
                src_ref=ref, dst_ref=ref, send_sem=rs.at[sidx(k), direction],
                recv_sem=rr.at[sidx(k), direction, 0],
                device_id={"expert": partner}, device_id_type=MESH,
            ).wait_send()
        ref = g_all.at[pl.ds(0, nz)] if k is None else buf.at[k, pl.ds(0, nz - 4)]
        pltpu.make_async_remote_copy(
            src_ref=ref, dst_ref=ref, send_sem=psd.at[sidx(k)], recv_sem=pr.at[sidx(k), 0],
            device_id={"expert": partner}, device_id_type=MESH,
        ).wait_send()

    def packed_sent(k, parity):
        for direction in range(2):
            packed_first(k, parity, direction).wait_send()
            packed_second(k, parity, direction).wait_send()
        ref = pin.at[k, 0, pl.ds(0, 2)]
        pltpu.make_async_remote_copy(
            src_ref=ref, dst_ref=ref, send_sem=pps.at[k], recv_sem=pr.at[k, 0],
            device_id={"expert": partner}, device_id_type=MESH,
        ).wait_send()

    ring_sent(None, 0)
    for k in range(items):
        ring_sent(k, k % 2)
        packed_sent(k, k % 2)
    w_sent()

    for q in range(NQ):
        r_all(q).wait_recv()
        total = land[q, 0].astype(F32)
        for i in range(1, ndp):
            total = total + land[q, i].astype(F32)
        grad_ref[:, q * cw : (q + 1) * cw] = total

    for q in range(NQ):
        r_all(q).wait_send()


def grad_kernel(mesh, tokens, cotangent, routes_t, gates_t, weight):
    ndp = mesh.shape["dp"]
    ne = mesh.shape["expert"]
    nz = ne // 2
    toks, width = tokens.shape
    cw = width // NQ
    fd = weight.shape[1]
    items = 2 * NQ
    hops = nz // 2 + 1
    nrows = ne * MOST
    dma = pltpu.SemaphoreType.DMA
    anywhere = pl.BlockSpec(memory_space=pl.ANY)
    vmem = pl.BlockSpec(memory_space=pltpu.VMEM)
    return pl.pallas_call(
        functools.partial(kernel, ndp, ne),
        out_shape=jax.ShapeDtypeStruct((fd, width), F32),
        in_specs=[anywhere, anywhere, vmem, vmem, anywhere],
        out_specs=vmem,
        scratch_shapes=[
            pltpu.VMEM((items, ne, toks, cw), BF16),
            pltpu.VMEM((2, ndp, fd, width), BF16),
            pltpu.VMEM((ne, ne, toks), F32),
            pltpu.VMEM((nz, 2 * MOST, 2 * toks), BF16),
            pltpu.VMEM((nz, 2 * MOST, 128), F32),
            pltpu.VMEM((items, nrows, cw), BF16),
            pltpu.VMEM((ndp * fd, nrows), BF16),
            pltpu.VMEM((NQ, ndp, fd, cw), BF16),
            pltpu.VMEM((NQ, ndp, fd, cw), BF16),
            pltpu.VMEM((2, 2, 4 * MOST, toks), BF16),
            pltpu.VMEM((items, 2, 2, 2 * MOST, cw), BF16),
            pltpu.VMEM((items, 2, 3, 2, 2 * MOST, cw), BF16),
            dma((items + 1,)),
            dma((items + 1, 2, hops)),
            dma((items + 1, 2)),
            dma((items + 1, nz)),
            dma((items + 1,)),
            dma((2, ndp, 2)),
            dma,
            dma((NQ,)),
            dma((NQ,)),
            dma((items, 2)),
            dma((items, 2)),
            dma((items,)),
        ],
        compiler_params=pltpu.CompilerParams(
            collective_id=0, has_side_effects=True, vmem_limit_bytes=67043328
        ),
        name="expert_grad",
    )(tokens, cotangent, routes_t, gates_t, weight)


def solution(mesh):
    def per_device(
        tokens, cotangent, routes, slot_gates, gate_up_weight, down_master, first_moment, second_moment
    ):
        grad = grad_kernel(
            mesh, tokens, cotangent, routes.T, slot_gates.T, jnp.swapaxes(gate_up_weight[0], 1, 2)
        )
        master = down_master[0]
        new_first = BETA_ONE * first_moment[0] + (1.0 - BETA_ONE) * grad
        new_second = BETA_TWO * second_moment[0] + (1.0 - BETA_TWO) * grad * grad
        new_down = master - LEARN_RATE * (
            new_first / (jnp.sqrt(new_second) + ADAM_EPS) + DECAY_RATE * master
        )
        return (new_down[None], new_first[None], new_second[None])

    return jax.shard_map(
        per_device,
        mesh=mesh,
        in_specs=(
            P(("dp", "expert"), None),
            P(("dp", "expert"), None),
            P(("dp", "expert"), None),
            P(("dp", "expert"), None),
            P("expert", None, None, "dp"),
            P("expert", "dp", None),
            P("expert", "dp", None),
            P("expert", "dp", None),
        ),
        out_specs=(P("expert", "dp", None), P("expert", "dp", None), P("expert", "dp", None)),
        check_vma=False,
    )
```

```python
import functools

import jax
import jax.numpy as jnp
from jax import lax
from jax.experimental import pallas as pl
from jax.experimental.pallas import tpu as pltpu
from jax.sharding import PartitionSpec as P

MOST = 24
NQ = 4
LAG = 1
SIDE = 4
PEER_ORDER = (
    (0, 1), (1, 0), (0, -1), (-1, 0), (1, 1), (-1, -1), (1, -1), (-1, 1),
    (0, 2), (2, 0), (1, 2), (2, 1), (-1, 2), (2, -1), (2, 2),
)

BETA_ONE = 0.9
BETA_TWO = 0.95
LEARN_RATE = 0.003
DECAY_RATE = 0.1
ADAM_EPS = 1e-08

MESH = pl.DeviceIdType.MESH
F32 = jnp.float32
BF16 = jnp.bfloat16


def kernel(
    ndp, ne,
    x_ref, c_ref, rt_ref, gt_ref, w_ref,
    grad_ref,
    buf, w_all, g_all, p_all, gate_all, rows, ht, ps, land, pm, po, pin,
    loc_sem, rr, rs, pr, psd, wr, ws, lr_sem, ls_sem, pos, pfs, pps,
):
    nz = ne // 2
    items = 2 * NQ
    hops = nz // 2 + 1
    toks = buf.shape[2]
    cw = buf.shape[3]
    width = NQ * cw
    pair = 2 * MOST
    nrows = nz * pair
    fd = w_ref.shape[1]
    ff = ndp * fd
    side = SIDE

    me = lax.axis_index("expert")
    dp = lax.axis_index("dp")
    z = me // 2
    core = me % 2
    partner = me + 1 - 2 * core

    def zslot(d):
        return 2 * ((z + d + nz) % nz) + core

    def load(k, t, q):
        src = x_ref if t == 0 else c_ref
        return pltpu.make_async_copy(
            src.at[:, pl.ds(q * cw, cw)], buf.at[k, me], loc_sem.at[k]
        )

    for t in range(2):
        for q in range(NQ):
            load(t * NQ + q, t, q).start()
    w_load = pltpu.make_async_copy(w_ref, w_all.at[:, dp], loc_sem.at[items])
    w_load.start()

    expert_id = lax.broadcasted_iota(jnp.int32, (ne, toks), 0)
    table = jnp.zeros((ne, toks), F32)
    for k in range(rt_ref.shape[0]):
        table = table + jnp.where(rt_ref[k : k + 1, :] == expert_id, gt_ref[k : k + 1, :], 0.0)
    g_all[me] = table

    barrier = pltpu.get_barrier_semaphore()
    for other in (zslot(1), zslot(-1), partner):
        pl.semaphore_signal(barrier, inc=1, device_id={"expert": other}, device_id_type=MESH)

    @pl.loop(1, ndp)
    def _(d):
        pl.semaphore_signal(
            barrier, inc=1, device_id={"dp": (dp + d) % ndp}, device_id_type=MESH
        )

    pl.semaphore_wait(barrier, 3 + ndp - 1)

    def chunk(k, s):
        return g_all.at[s] if k is None else buf.at[k, s]

    def sidx(k):
        return items if k is None else k

    def ring_copy(k, direction, s, h):
        return pltpu.make_async_remote_copy(
            src_ref=chunk(k, s), dst_ref=chunk(k, s),
            send_sem=rs.at[sidx(k), direction],
            recv_sem=rr.at[sidx(k), direction, h + 1],
            device_id={"expert": zslot(1 if direction == 0 else -1)},
            device_id_type=MESH,
        )

    def ring_arrived(k, direction, s, h):
        pltpu.make_async_remote_copy(
            src_ref=chunk(k, s), dst_ref=chunk(k, s),
            send_sem=rs.at[sidx(k), direction],
            recv_sem=rr.at[sidx(k), direction, h],
            device_id={"expert": zslot(1 if direction == 0 else -1)},
            device_id_type=MESH,
        ).wait_recv()

    def partner_copy(k, s, zz):
        return pltpu.make_async_remote_copy(
            src_ref=chunk(k, s), dst_ref=chunk(k, s),
            send_sem=psd.at[sidx(k)], recv_sem=pr.at[sidx(k), zz],
            device_id={"expert": partner}, device_id_type=MESH,
        )

    def reach(parity, direction):
        return nz // 2 if parity == direction else nz // 2 - 1

    def full_reach(k, parity, direction):
        return reach(parity, direction) - (0 if k is None else 2)

    def packed_copy(k, direction, src, dst, sem, h):
        return pltpu.make_async_remote_copy(
            src_ref=src, dst_ref=dst, send_sem=sem.at[k, direction],
            recv_sem=rr.at[k, direction, h],
            device_id={"expert": zslot(1 if direction == 0 else -1)},
            device_id_type=MESH,
        )

    def packed_first(k, parity, direction):
        return packed_copy(
            k, direction, po.at[k, direction], pin.at[k, direction, pl.ds(0, 2), core],
            pos, reach(parity, direction) - 1,
        )

    def packed_second(k, parity, direction):
        return packed_copy(
            k, direction, pin.at[k, direction, 1, core], pin.at[k, direction, 2, core],
            pfs, reach(parity, direction),
        )

    def packed_partner(k, direction, slot, zz, side_core):
        ref = pin.at[k, direction, slot, side_core]
        return pltpu.make_async_remote_copy(
            src_ref=ref, dst_ref=ref, send_sem=pps.at[k], recv_sem=pr.at[k, zz],
            device_id={"expert": partner}, device_id_type=MESH,
        )

    def event(k, parity, h, ready):
        @pl.when(h == 0)
        def _():
            ready()
            ring_copy(k, 0, me, 0).start()
            ring_copy(k, 1, me, 0).start()
            partner_copy(k, me, z).start()

        for direction in range(2):
            last = full_reach(k, parity, direction)
            s = zslot(-h if direction == 0 else h)

            @pl.when((h > 0) & (h <= last))
            def _():
                ring_arrived(k, direction, s, h)

                @pl.when(h < last)
                def _():
                    ring_copy(k, direction, s, h).start()

                partner_copy(k, s, s // 2).start()

            if k is not None:
                @pl.when(h == last)
                def _():
                    few = jnp.dot(
                        pm[direction, int(parity == direction)], buf[k, s],
                        preferred_element_type=F32,
                    )
                    po[k, direction] = few.astype(BF16).reshape(2, pair, cw)

                @pl.when(h == last + 1)
                def _():
                    packed_first(k, parity, direction).wait_recv()
                    packed_second(k, parity, direction).start()
                    packed_partner(k, direction, 0, s // 2, core).start()

                @pl.when(h == last + 2)
                def _():
                    packed_second(k, parity, direction).wait_recv()
                    packed_partner(k, direction, 2, s // 2, core).start()

    def send_packed(k, parity, h):
        for direction in range(2):
            @pl.when(h == full_reach(k, parity, direction))
            def _():
                packed_first(k, parity, direction).start()

    def pairs(k, parity, h, work, packed_work):
        def one(zz):
            partner_copy(k, 2 * zz + 1 - core, zz).wait_recv()
            work(zz)

        @pl.when(h == 0)
        def _():
            one(z)

        for direction in range(2):
            last = full_reach(k, parity, direction)
            zz = zslot(-h if direction == 0 else h) // 2

            @pl.when((h > 0) & (h <= last))
            def _():
                one(zz)

            if k is not None:
                for slot in (0, 2):
                    @pl.when(h == last + 1 + slot // 2)
                    def _():
                        packed_partner(k, direction, slot, zz, 1 - core).wait_recv()
                        packed_work(zz, direction, slot)

    def ranks(mask):
        row_id = lax.broadcasted_iota(jnp.int32, (toks, toks), 0)
        col_id = lax.broadcasted_iota(jnp.int32, (toks, toks), 1)
        before = jnp.where(row_id < col_id, 1.0, 0.0).astype(BF16)
        padded = jnp.concatenate([mask, jnp.zeros((8 - mask.shape[0], toks), F32)], axis=0)
        return jnp.dot(padded.astype(BF16), before, preferred_element_type=F32)

    def build_pack(direction, long, s):
        parts = []
        for ahead in (1, 2):
            dest = zslot(ahead if direction == 0 else -ahead) // 2
            for other in range(2):
                parts.append(g_all[s, pl.ds(2 * dest + other, 1), :])
        mask = jnp.where(jnp.concatenate(parts, axis=0) > 0.0, 1.0, 0.0)
        rank = ranks(mask)
        wanted = lax.broadcasted_iota(jnp.int32, (2 * pair, toks), 0).astype(F32)
        total = jnp.zeros((2 * pair, toks), F32)
        for i in range(4):
            place = jnp.where(mask[i : i + 1, :] > 0.0, rank[i : i + 1, :] + float(MOST * i), -1.0)
            total = total + jnp.where(wanted == place, 1.0, 0.0)
        pm[direction, long] = total.astype(BF16)

    def build(zz):
        both = jnp.concatenate(
            [g_all[2 * zz, pl.ds(me, 1), :], g_all[2 * zz + 1, pl.ds(me, 1), :]], axis=0
        )
        mask = jnp.where(both > 0.0, 1.0, 0.0)
        rank = ranks(mask)
        places = []
        for s in range(2):
            places.append(
                jnp.where(mask[s : s + 1, :] > 0.0, rank[s : s + 1, :] + float(MOST * s), -1.0)
            )
        place = jnp.concatenate(places, axis=1)
        gates = jnp.concatenate([both[0:1, :], both[1:2, :]], axis=1)
        wanted = lax.broadcasted_iota(jnp.int32, (pair, 2 * toks), 0).astype(F32)
        hit = wanted == place
        p_all[zz] = jnp.where(hit, 1.0, 0.0).astype(BF16)
        gate = jnp.sum(jnp.where(hit, gates, 0.0), axis=1, keepdims=True)
        gate_all[zz] = jnp.broadcast_to(gate, (pair, 128))

    def keep(k, zz, got):
        gate = gate_all[zz][:, 0:1]
        scale = jnp.where(k >= NQ, gate, jnp.ones_like(gate))
        rows[k, pl.ds(pl.multiple_of(zz * pair, 16), pair), :] = (got * scale).astype(BF16)

    def select(k, zz):
        both = buf[k, pl.ds(2 * zz, 2)].reshape(2 * toks, cw)
        keep(k, zz, jnp.dot(p_all[zz], both, preferred_element_type=F32))

    def select_packed(k, zz, direction, slot):
        both = pin[k, direction, slot].reshape(2 * pair, cw)
        to = lax.broadcasted_iota(jnp.int32, (pair, 2 * pair), 0)
        of = lax.broadcasted_iota(jnp.int32, (pair, 2 * pair), 1)
        mine = to + MOST * core + jnp.where(to >= MOST, MOST, 0)
        pick = jnp.where(of == mine, 1.0, 0.0).astype(BF16)
        keep(k, zz, jnp.dot(pick, both, preferred_element_type=F32))

    fsplit = 2
    fb = ff // fsplit
    rb = 256 if nrows % 256 == 0 else nrows
    rsplit = nrows // rb
    pieces = fsplit * rsplit

    def nt(a, b):
        return lax.dot_general(a, b, (((1,), (1,)), ((), ())), preferred_element_type=F32)

    def hidden_piece(p):
        f0 = p // rsplit
        r0 = p % rsplit
        gate = jnp.zeros((fb, rb), F32)
        up = jnp.zeros((fb, rb), F32)
        for q in range(NQ):
            xs = rows[q, pl.ds(pl.multiple_of(r0 * rb, 16), rb), :]
            blocks = pl.ds(f0 * (ndp // fsplit), ndp // fsplit)
            cols = pl.ds(q * cw, cw)
            gate = gate + nt(w_all[0, blocks, :, cols].reshape(fb, cw), xs)
            up = up + nt(w_all[1, blocks, :, cols].reshape(fb, cw), xs)
        act = gate / (1.0 + jnp.exp(-gate)) * up
        ht[pl.ds(pl.multiple_of(f0 * fb, 16), fb), pl.ds(pl.multiple_of(r0 * rb, 128), rb)] = act.astype(BF16)

    def offset_peer(u, v):
        return ((dp // side + u + side) % side) * side + (dp % side + v + side) % side

    def w_copy(p, slot, half, u, v):
        ref = w_all.at[p, slot]
        if half is not None:
            ref = w_all.at[p, slot, :, pl.ds(half * (width // 2), width // 2)]
        return pltpu.make_async_remote_copy(
            src_ref=ref, dst_ref=ref, send_sem=ws, recv_sem=wr.at[p, slot, half or 0],
            device_id={"dp": offset_peer(u, v)}, device_id_type=MESH,
        )

    def w_hop(p, axis, slot, half, step):
        along_x = (p == 0) == (axis == 0)
        return w_copy(p, slot, half, step if along_x else 0, 0 if along_x else step)

    def w_slot(p, u, v):
        return offset_peer(u, v) if p == 0 else offset_peer(v, u)

    def w_step(n):
        for p in range(2):
            if n == 0:
                for axis in range(2):
                    for step in (1, -1):
                        w_hop(p, axis, dp, None, step).start()
                continue
            if n == 1:
                for step in (1, -1):
                    slot = w_slot(p, -step, 0)
                    w_hop(p, 0, slot, None, step).wait_recv()
                    w_hop(p, 0, slot, 0 if step == 1 else 1, step).start()
                    for step2 in (1, -1):
                        w_hop(p, 1, slot, None, step2).start()
            if n == 2:
                slot = w_slot(p, 2, 0)
                for half in range(2):
                    w_hop(p, 0, slot, half, 1).wait_recv()
                for step2 in (1, -1):
                    w_hop(p, 1, slot, None, step2).start()
            for u in ((0,), (1, -1), (2,))[n - 1] if n < 4 else ():
                for step in (1, -1):
                    slot = w_slot(p, u, -step)
                    w_hop(p, 1, slot, None, step).wait_recv()
                    w_hop(p, 1, slot, 0 if step == 1 else 1, step).start()
            if n == 4:
                for u in (0, 1, -1, 2):
                    for half in range(2):
                        w_hop(p, 1, w_slot(p, u, 2), half, 1).wait_recv()

    def w_sent():
        ref = w_all.at[:, pl.ds(0, ndp - 1)]
        pltpu.make_async_remote_copy(
            src_ref=ref, dst_ref=ref, send_sem=ws, recv_sem=wr.at[0, 0, 0],
            device_id={"dp": offset_peer(1, 0)}, device_id_type=MESH,
        ).wait_send()

    def r_copy(q, other):
        return pltpu.make_async_remote_copy(
            src_ref=ps.at[q, other], dst_ref=land.at[q, dp],
            send_sem=ls_sem.at[q], recv_sem=lr_sem.at[q],
            device_id={"dp": other}, device_id_type=MESH,
        )

    def r_all(q):
        return pltpu.make_async_remote_copy(
            src_ref=ps.at[q, pl.ds(0, ndp - 1)], dst_ref=land.at[q, pl.ds(0, ndp - 1)],
            send_sem=ls_sem.at[q], recv_sem=lr_sem.at[q],
            device_id={"dp": offset_peer(1, 0)}, device_id_type=MESH,
        )

    def partial(q):
        for f0 in range(fsplit):
            part = jnp.dot(
                ht[f0 * fb : (f0 + 1) * fb, :], rows[NQ + q], preferred_element_type=F32
            )
            per = ndp // fsplit
            ps[q, f0 * per : (f0 + 1) * per] = part.astype(BF16).reshape(per, fd, cw)
        land[q, dp] = ps[q, dp]

        for u, v in PEER_ORDER:
            r_copy(q, offset_peer(u, v)).start()

    lanes = items // 2
    c_start = max(hops - 4, 4)

    def begin(k):
        return (k // NQ) * (c_start + ((k - NQ) * 2))

    last_round = c_start + ((NQ - 1) * 2) + hops

    def each(g, work):
        for parity in range(2):
            k = 2 * (g % lanes) + parity
            h = g // lanes - begin(k)

            @pl.when((g >= 0) & (h >= 0) & (h < hops))
            def _():
                work(k, parity, h)

    def compute(k, parity, h):
        pairs(k, parity, h, functools.partial(select, k), functools.partial(select_packed, k))

        @pl.when((h == hops - 1) & (k >= NQ))
        def _():
            partial(k - NQ)

    @pl.loop(0, last_round * lanes + LAG)
    def _(g):
        r = g // lanes
        m = g % lanes

        @pl.when((m == 0) & (r < hops))
        def _():
            event(None, 0, r, lambda: None)

        for direction in range(2):
            for long in range(2):
                h = nz // 2 - 3 + long

                @pl.when((m == 0) & (r == h))
                def _():
                    build_pack(direction, long, zslot(-h if direction == 0 else h))

        each(g, lambda k, parity, h: event(k, parity, h, lambda: load(k, 0, 0).wait()))

        @pl.when((m == LAG) & (r < hops))
        def _():
            pairs(None, 0, r, build, None)

        each(g - LAG, compute)
        each(g, send_packed)

        for n in range(4):
            @pl.when((m == lanes - 1) & (r == n))
            def _():
                if n == 0:
                    w_load.wait()
                w_step(n)

        @pl.when((m == lanes // 2 - 1) & (r == hops + 1))
        def _():
            w_step(4)

        piece = 2 * (r - hops - 1) + m // (lanes // 2)

        @pl.when((m % (lanes // 2) == lanes // 2 - 1) & (r > hops) & (piece < pieces))
        def _():
            hidden_piece(piece)

    def ring_sent(k, parity):
        for direction in range(2):
            count = pl.ds(0, full_reach(k, parity, direction))
            ref = g_all.at[count] if k is None else buf.at[k, count]
            pltpu.make_async_remote_copy(
                src_ref=ref, dst_ref=ref, send_sem=rs.at[sidx(k), direction],
                recv_sem=rr.at[sidx(k), direction, 0],
                device_id={"expert": partner}, device_id_type=MESH,
            ).wait_send()
        ref = g_all.at[pl.ds(0, nz)] if k is None else buf.at[k, pl.ds(0, nz - 4)]
        pltpu.make_async_remote_copy(
            src_ref=ref, dst_ref=ref, send_sem=psd.at[sidx(k)], recv_sem=pr.at[sidx(k), 0],
            device_id={"expert": partner}, device_id_type=MESH,
        ).wait_send()

    def packed_sent(k, parity):
        for direction in range(2):
            packed_first(k, parity, direction).wait_send()
            packed_second(k, parity, direction).wait_send()
        ref = pin.at[k, 0, pl.ds(0, 2)]
        pltpu.make_async_remote_copy(
            src_ref=ref, dst_ref=ref, send_sem=pps.at[k], recv_sem=pr.at[k, 0],
            device_id={"expert": partner}, device_id_type=MESH,
        ).wait_send()

    ring_sent(None, 0)

    @pl.loop(0, lanes)
    def _(m):
        for parity in range(2):
            ring_sent(2 * m + parity, parity)
            packed_sent(2 * m + parity, parity)

    w_sent()

    @pl.loop(0, NQ)
    def _(q):
        r_all(q).wait_recv()
        total = land[q, 0].astype(F32)
        for i in range(1, ndp):
            total = total + land[q, i].astype(F32)
        grad_ref[:, pl.ds(pl.multiple_of(q * cw, 128), cw)] = total

    @pl.loop(0, NQ)
    def _(q):
        r_all(q).wait_send()


def grad_kernel(mesh, tokens, cotangent, routes_t, gates_t, weight):
    ndp = mesh.shape["dp"]
    ne = mesh.shape["expert"]
    nz = ne // 2
    toks, width = tokens.shape
    cw = width // NQ
    fd = weight.shape[1]
    items = 2 * NQ
    hops = nz // 2 + 1
    nrows = ne * MOST
    dma = pltpu.SemaphoreType.DMA
    anywhere = pl.BlockSpec(memory_space=pl.ANY)
    vmem = pl.BlockSpec(memory_space=pltpu.VMEM)
    return pl.pallas_call(
        functools.partial(kernel, ndp, ne),
        out_shape=jax.ShapeDtypeStruct((fd, width), F32),
        in_specs=[anywhere, anywhere, vmem, vmem, anywhere],
        out_specs=vmem,
        scratch_shapes=[
            pltpu.VMEM((items, ne, toks, cw), BF16),
            pltpu.VMEM((2, ndp, fd, width), BF16),
            pltpu.VMEM((ne, ne, toks), F32),
            pltpu.VMEM((nz, 2 * MOST, 2 * toks), BF16),
            pltpu.VMEM((nz, 2 * MOST, 128), F32),
            pltpu.VMEM((items, nrows, cw), BF16),
            pltpu.VMEM((ndp * fd, nrows), BF16),
            pltpu.VMEM((NQ, ndp, fd, cw), BF16),
            pltpu.VMEM((NQ, ndp, fd, cw), BF16),
            pltpu.VMEM((2, 2, 4 * MOST, toks), BF16),
            pltpu.VMEM((items, 2, 2, 2 * MOST, cw), BF16),
            pltpu.VMEM((items, 2, 3, 2, 2 * MOST, cw), BF16),
            dma((items + 1,)),
            dma((items + 1, 2, hops)),
            dma((items + 1, 2)),
            dma((items + 1, nz)),
            dma((items + 1,)),
            dma((2, ndp, 2)),
            dma,
            dma((NQ,)),
            dma((NQ,)),
            dma((items, 2)),
            dma((items, 2)),
            dma((items,)),
        ],
        compiler_params=pltpu.CompilerParams(
            collective_id=0, has_side_effects=True, vmem_limit_bytes=67043328
        ),
        name="expert_grad",
    )(tokens, cotangent, routes_t, gates_t, weight)


def solution(mesh):
    def per_device(
        tokens, cotangent, routes, slot_gates, gate_up_weight, down_master, first_moment, second_moment
    ):
        grad = grad_kernel(
            mesh, tokens, cotangent, routes.T, slot_gates.T, jnp.swapaxes(gate_up_weight[0], 1, 2)
        )
        master = down_master[0]
        new_first = BETA_ONE * first_moment[0] + (1.0 - BETA_ONE) * grad
        new_second = BETA_TWO * second_moment[0] + (1.0 - BETA_TWO) * grad * grad
        new_down = master - LEARN_RATE * (
            new_first / (jnp.sqrt(new_second) + ADAM_EPS) + DECAY_RATE * master
        )
        return (new_down[None], new_first[None], new_second[None])

    return jax.shard_map(
        per_device,
        mesh=mesh,
        in_specs=(
            P(("dp", "expert"), None),
            P(("dp", "expert"), None),
            P(("dp", "expert"), None),
            P(("dp", "expert"), None),
            P("expert", None, None, "dp"),
            P("expert", "dp", None),
            P("expert", "dp", None),
            P("expert", "dp", None),
        ),
        out_specs=(P("expert", "dp", None), P("expert", "dp", None), P("expert", "dp", None)),
        check_vma=False,
    )
```

```python
import functools

import jax
import jax.numpy as jnp
from jax import lax
from jax.experimental import pallas as pl
from jax.experimental.pallas import tpu as pltpu
from jax.sharding import PartitionSpec as P

MOST = 24
NQ = 4
LAG = 1
SIDE = 4

BETA_ONE = 0.9
BETA_TWO = 0.95
LEARN_RATE = 0.003
DECAY_RATE = 0.1
ADAM_EPS = 1e-08

MESH = pl.DeviceIdType.MESH
F32 = jnp.float32
BF16 = jnp.bfloat16


def kernel(
    ndp, ne,
    x_ref, c_ref, rt_ref, gt_ref, w_ref,
    grad_ref,
    buf, w_all, g_all, p_all, gate_all, rows, ht, ps, land, pm, po, pin,
    loc_sem, rr, rs, pr, psd, wr, ws, lr_sem, ls_sem, pos, pfs, pps,
):
    nz = ne // 2
    items = 2 * NQ
    hops = nz // 2 + 1
    toks = buf.shape[2]
    cw = buf.shape[3]
    width = NQ * cw
    pair = 2 * MOST
    nrows = nz * pair
    fd = w_ref.shape[1]
    ff = ndp * fd
    side = SIDE

    me = lax.axis_index("expert")
    dp = lax.axis_index("dp")
    z = me // 2
    core = me % 2
    partner = me + 1 - 2 * core

    def zslot(d):
        return 2 * ((z + d + nz) % nz) + core

    def load(k, t, q):
        src = x_ref if t == 0 else c_ref
        return pltpu.make_async_copy(
            src.at[:, pl.ds(q * cw, cw)], buf.at[k, me], loc_sem.at[k]
        )

    for t in range(2):
        for q in range(NQ):
            load(t * NQ + q, t, q).start()
    w_load = pltpu.make_async_copy(w_ref, w_all.at[:, dp], loc_sem.at[items])
    w_load.start()

    expert_id = lax.broadcasted_iota(jnp.int32, (ne, toks), 0)
    table = jnp.zeros((ne, toks), F32)
    for k in range(rt_ref.shape[0]):
        table = table + jnp.where(rt_ref[k : k + 1, :] == expert_id, gt_ref[k : k + 1, :], 0.0)
    g_all[me] = table

    barrier = pltpu.get_barrier_semaphore()
    for other in (zslot(1), zslot(-1), partner):
        pl.semaphore_signal(barrier, inc=1, device_id={"expert": other}, device_id_type=MESH)

    @pl.loop(1, ndp)
    def _(d):
        pl.semaphore_signal(
            barrier, inc=1, device_id={"dp": (dp + d) % ndp}, device_id_type=MESH
        )

    pl.semaphore_wait(barrier, 3 + ndp - 1)

    def chunk(k, s):
        return g_all.at[s] if k is None else buf.at[k, s]

    def sidx(k):
        return items if k is None else k

    def ring_copy(k, direction, s, h):
        return pltpu.make_async_remote_copy(
            src_ref=chunk(k, s), dst_ref=chunk(k, s),
            send_sem=rs.at[sidx(k), direction],
            recv_sem=rr.at[sidx(k), direction, h + 1],
            device_id={"expert": zslot(1 if direction == 0 else -1)},
            device_id_type=MESH,
        )

    def ring_arrived(k, direction, s, h):
        pltpu.make_async_remote_copy(
            src_ref=chunk(k, s), dst_ref=chunk(k, s),
            send_sem=rs.at[sidx(k), direction],
            recv_sem=rr.at[sidx(k), direction, h],
            device_id={"expert": zslot(1 if direction == 0 else -1)},
            device_id_type=MESH,
        ).wait_recv()

    def partner_copy(k, s, zz):
        return pltpu.make_async_remote_copy(
            src_ref=chunk(k, s), dst_ref=chunk(k, s),
            send_sem=psd.at[sidx(k)], recv_sem=pr.at[sidx(k), zz],
            device_id={"expert": partner}, device_id_type=MESH,
        )

    def reach(parity, direction):
        return nz // 2 if parity == direction else nz // 2 - 1

    def full_reach(k, parity, direction):
        return reach(parity, direction) - (0 if k is None else 2)

    def packed_copy(k, direction, src, dst, sem, h):
        return pltpu.make_async_remote_copy(
            src_ref=src, dst_ref=dst, send_sem=sem.at[k, direction],
            recv_sem=rr.at[k, direction, h],
            device_id={"expert": zslot(1 if direction == 0 else -1)},
            device_id_type=MESH,
        )

    def packed_first(k, parity, direction):
        return packed_copy(
            k, direction, po.at[k, direction], pin.at[k, direction, pl.ds(0, 2), core],
            pos, reach(parity, direction) - 1,
        )

    def packed_second(k, parity, direction):
        return packed_copy(
            k, direction, pin.at[k, direction, 1, core], pin.at[k, direction, 2, core],
            pfs, reach(parity, direction),
        )

    def packed_partner(k, direction, slot, zz, side_core):
        ref = pin.at[k, direction, slot, side_core]
        return pltpu.make_async_remote_copy(
            src_ref=ref, dst_ref=ref, send_sem=pps.at[k], recv_sem=pr.at[k, zz],
            device_id={"expert": partner}, device_id_type=MESH,
        )

    def event(k, parity, h, ready):
        @pl.when(h == 0)
        def _():
            ready()
            ring_copy(k, 0, me, 0).start()
            ring_copy(k, 1, me, 0).start()
            partner_copy(k, me, z).start()

        for direction in range(2):
            last = full_reach(k, parity, direction)
            s = zslot(-h if direction == 0 else h)

            @pl.when((h > 0) & (h <= last))
            def _():
                ring_arrived(k, direction, s, h)

                @pl.when(h < last)
                def _():
                    ring_copy(k, direction, s, h).start()

                partner_copy(k, s, s // 2).start()

            if k is not None:
                @pl.when(h == last)
                def _():
                    few = jnp.dot(
                        pm[direction, int(parity == direction)], buf[k, s],
                        preferred_element_type=F32,
                    )
                    po[k, direction] = few.astype(BF16).reshape(2, pair, cw)

                @pl.when(h == last + 1)
                def _():
                    packed_first(k, parity, direction).wait_recv()
                    packed_second(k, parity, direction).start()
                    packed_partner(k, direction, 0, s // 2, core).start()

                @pl.when(h == last + 2)
                def _():
                    packed_second(k, parity, direction).wait_recv()
                    packed_partner(k, direction, 2, s // 2, core).start()

    def send_packed(k, parity, h):
        for direction in range(2):
            @pl.when(h == full_reach(k, parity, direction))
            def _():
                packed_first(k, parity, direction).start()

    def pairs(k, parity, h, work, packed_work):
        def one(zz):
            partner_copy(k, 2 * zz + 1 - core, zz).wait_recv()
            work(zz)

        @pl.when(h == 0)
        def _():
            one(z)

        for direction in range(2):
            last = full_reach(k, parity, direction)
            zz = zslot(-h if direction == 0 else h) // 2

            @pl.when((h > 0) & (h <= last))
            def _():
                one(zz)

            if k is not None:
                for slot in (0, 2):
                    @pl.when(h == last + 1 + slot // 2)
                    def _():
                        packed_partner(k, direction, slot, zz, 1 - core).wait_recv()
                        packed_work(zz, direction, slot)

    def ranks(mask):
        row_id = lax.broadcasted_iota(jnp.int32, (toks, toks), 0)
        col_id = lax.broadcasted_iota(jnp.int32, (toks, toks), 1)
        before = jnp.where(row_id < col_id, 1.0, 0.0).astype(BF16)
        padded = jnp.concatenate([mask, jnp.zeros((8 - mask.shape[0], toks), F32)], axis=0)
        return jnp.dot(padded.astype(BF16), before, preferred_element_type=F32)

    def build_pack(direction, long, s):
        parts = []
        for ahead in (1, 2):
            dest = zslot(ahead if direction == 0 else -ahead) // 2
            for other in range(2):
                parts.append(g_all[s, pl.ds(2 * dest + other, 1), :])
        mask = jnp.where(jnp.concatenate(parts, axis=0) > 0.0, 1.0, 0.0)
        rank = ranks(mask)
        wanted = lax.broadcasted_iota(jnp.int32, (2 * pair, toks), 0).astype(F32)
        total = jnp.zeros((2 * pair, toks), F32)
        for i in range(4):
            place = jnp.where(mask[i : i + 1, :] > 0.0, rank[i : i + 1, :] + float(MOST * i), -1.0)
            total = total + jnp.where(wanted == place, 1.0, 0.0)
        pm[direction, long] = total.astype(BF16)

    def build(zz):
        both = jnp.concatenate(
            [g_all[2 * zz, pl.ds(me, 1), :], g_all[2 * zz + 1, pl.ds(me, 1), :]], axis=0
        )
        mask = jnp.where(both > 0.0, 1.0, 0.0)
        rank = ranks(mask)
        places = []
        for s in range(2):
            places.append(
                jnp.where(mask[s : s + 1, :] > 0.0, rank[s : s + 1, :] + float(MOST * s), -1.0)
            )
        place = jnp.concatenate(places, axis=1)
        gates = jnp.concatenate([both[0:1, :], both[1:2, :]], axis=1)
        wanted = lax.broadcasted_iota(jnp.int32, (pair, 2 * toks), 0).astype(F32)
        hit = wanted == place
        p_all[zz] = jnp.where(hit, 1.0, 0.0).astype(BF16)
        gate = jnp.sum(jnp.where(hit, gates, 0.0), axis=1, keepdims=True)
        gate_all[zz] = jnp.broadcast_to(gate, (pair, 128))

    def keep(k, zz, got):
        gate = gate_all[zz][:, 0:1]
        scale = jnp.where(k >= NQ, gate, jnp.ones_like(gate))
        rows[k, pl.ds(pl.multiple_of(zz * pair, 16), pair), :] = (got * scale).astype(BF16)

    def select(k, zz):
        both = buf[k, pl.ds(2 * zz, 2)].reshape(2 * toks, cw)
        keep(k, zz, jnp.dot(p_all[zz], both, preferred_element_type=F32))

    def select_packed(k, zz, direction, slot):
        both = pin[k, direction, slot].reshape(2 * pair, cw)
        to = lax.broadcasted_iota(jnp.int32, (pair, 2 * pair), 0)
        of = lax.broadcasted_iota(jnp.int32, (pair, 2 * pair), 1)
        mine = to + MOST * core + jnp.where(to >= MOST, MOST, 0)
        pick = jnp.where(of == mine, 1.0, 0.0).astype(BF16)
        keep(k, zz, jnp.dot(pick, both, preferred_element_type=F32))

    fsplit = 2
    fb = ff // fsplit
    rb = 256 if nrows % 256 == 0 else nrows
    rsplit = nrows // rb
    pieces = fsplit * rsplit

    def nt(a, b):
        return lax.dot_general(a, b, (((1,), (1,)), ((), ())), preferred_element_type=F32)

    def hidden_piece(p):
        f0 = p // rsplit
        r0 = p % rsplit
        gate = jnp.zeros((fb, rb), F32)
        up = jnp.zeros((fb, rb), F32)
        for q in range(NQ):
            xs = rows[q, pl.ds(pl.multiple_of(r0 * rb, 16), rb), :]
            blocks = pl.ds(f0 * (ndp // fsplit), ndp // fsplit)
            cols = pl.ds(q * cw, cw)
            gate = gate + nt(w_all[0, blocks, :, cols].reshape(fb, cw), xs)
            up = up + nt(w_all[1, blocks, :, cols].reshape(fb, cw), xs)
        act = gate / (1.0 + jnp.exp(-gate)) * up
        ht[pl.ds(pl.multiple_of(f0 * fb, 16), fb), pl.ds(pl.multiple_of(r0 * rb, 128), rb)] = act.astype(BF16)

    def offset_peer(u, v):
        return ((dp // side + u + side) % side) * side + (dp % side + v + side) % side

    def w_copy(p, slot, half, u, v):
        ref = w_all.at[p, slot]
        if half is not None:
            ref = w_all.at[p, slot, :, pl.ds(half * (width // 2), width // 2)]
        return pltpu.make_async_remote_copy(
            src_ref=ref, dst_ref=ref, send_sem=ws, recv_sem=wr.at[p, slot, half or 0],
            device_id={"dp": offset_peer(u, v)}, device_id_type=MESH,
        )

    def w_hop(p, axis, slot, half, step):
        along_x = (p == 0) == (axis == 0)
        return w_copy(p, slot, half, step if along_x else 0, 0 if along_x else step)

    def w_slot(p, u, v):
        return offset_peer(u, v) if p == 0 else offset_peer(v, u)

    def w_step(n):
        for p in range(2):
            if n == 0:
                for axis in range(2):
                    for step in (1, -1):
                        w_hop(p, axis, dp, None, step).start()
                continue
            if n == 1:
                for step in (1, -1):
                    slot = w_slot(p, -step, 0)
                    w_hop(p, 0, slot, None, step).wait_recv()
                    w_hop(p, 0, slot, 0 if step == 1 else 1, step).start()
                    for step2 in (1, -1):
                        w_hop(p, 1, slot, None, step2).start()
            if n == 2:
                slot = w_slot(p, 2, 0)
                for half in range(2):
                    w_hop(p, 0, slot, half, 1).wait_recv()
                for step2 in (1, -1):
                    w_hop(p, 1, slot, None, step2).start()
            for u in ((0,), (1, -1), (2,))[n - 1] if n < 4 else ():
                for step in (1, -1):
                    slot = w_slot(p, u, -step)
                    w_hop(p, 1, slot, None, step).wait_recv()
                    w_hop(p, 1, slot, 0 if step == 1 else 1, step).start()
            if n == 4:
                for u in (0, 1, -1, 2):
                    for half in range(2):
                        w_hop(p, 1, w_slot(p, u, 2), half, 1).wait_recv()

    def w_sent():
        ref = w_all.at[:, pl.ds(0, ndp - 1)]
        pltpu.make_async_remote_copy(
            src_ref=ref, dst_ref=ref, send_sem=ws, recv_sem=wr.at[0, 0, 0],
            device_id={"dp": offset_peer(1, 0)}, device_id_type=MESH,
        ).wait_send()

    def r_copy(q, other):
        return pltpu.make_async_remote_copy(
            src_ref=ps.at[q, other], dst_ref=land.at[q, dp],
            send_sem=ls_sem.at[q], recv_sem=lr_sem.at[q],
            device_id={"dp": other}, device_id_type=MESH,
        )

    def r_all(q):
        return pltpu.make_async_remote_copy(
            src_ref=ps.at[q, pl.ds(0, ndp - 1)], dst_ref=land.at[q, pl.ds(0, ndp - 1)],
            send_sem=ls_sem.at[q], recv_sem=lr_sem.at[q],
            device_id={"dp": offset_peer(1, 0)}, device_id_type=MESH,
        )

    def partial(q):
        bl = side * fd
        for f in range(1, side + 2):
            if f <= side:
                row = (dp // side + f) % side
                part = jnp.dot(
                    ht[pl.ds(pl.multiple_of(row * bl, 16), bl), :], rows[NQ + q],
                    preferred_element_type=F32,
                )
                ps[q, pl.ds(row * side, side)] = part.astype(BF16).reshape(side, fd, cw)
            if f > 1:
                for v in (1, 2, 3, 0):
                    if f <= side or v:
                        r_copy(q, offset_peer((f - 1) % side, v)).start()
        land[q, dp] = ps[q, dp]

    lanes = items // 2
    c_start = max(hops - 4, 4)

    def begin(k):
        return (k // NQ) * (c_start + ((k - NQ) * 2))

    last_round = c_start + ((NQ - 1) * 2) + hops

    def each(g, work):
        for parity in range(2):
            k = 2 * (g % lanes) + parity
            h = g // lanes - begin(k)

            @pl.when((g >= 0) & (h >= 0) & (h < hops))
            def _():
                work(k, parity, h)

    def compute(k, parity, h):
        pairs(k, parity, h, functools.partial(select, k), functools.partial(select_packed, k))

        @pl.when((h == hops - 1) & (k >= NQ))
        def _():
            partial(k - NQ)

    @pl.loop(0, last_round * lanes + LAG)
    def _(g):
        r = g // lanes
        m = g % lanes

        @pl.when((m == 0) & (r < hops))
        def _():
            event(None, 0, r, lambda: None)

        for direction in range(2):
            for long in range(2):
                h = nz // 2 - 3 + long

                @pl.when((m == 0) & (r == h))
                def _():
                    build_pack(direction, long, zslot(-h if direction == 0 else h))

        each(g, lambda k, parity, h: event(k, parity, h, lambda: load(k, 0, 0).wait()))

        @pl.when((m == LAG) & (r < hops))
        def _():
            pairs(None, 0, r, build, None)

        each(g - LAG, compute)
        each(g, send_packed)

        for n in range(4):
            @pl.when((m == lanes - 1) & (r == n))
            def _():
                if n == 0:
                    w_load.wait()
                w_step(n)

        @pl.when((m == lanes // 2 - 1) & (r == hops + 1))
        def _():
            w_step(4)

        piece = 2 * (r - hops - 1) + m // (lanes // 2)

        @pl.when((m % (lanes // 2) == lanes // 2 - 1) & (r > hops) & (piece < pieces))
        def _():
            hidden_piece(piece)

    def ring_sent(k, parity):
        for direction in range(2):
            count = pl.ds(0, full_reach(k, parity, direction))
            ref = g_all.at[count] if k is None else buf.at[k, count]
            pltpu.make_async_remote_copy(
                src_ref=ref, dst_ref=ref, send_sem=rs.at[sidx(k), direction],
                recv_sem=rr.at[sidx(k), direction, 0],
                device_id={"expert": partner}, device_id_type=MESH,
            ).wait_send()
        ref = g_all.at[pl.ds(0, nz)] if k is None else buf.at[k, pl.ds(0, nz - 4)]
        pltpu.make_async_remote_copy(
            src_ref=ref, dst_ref=ref, send_sem=psd.at[sidx(k)], recv_sem=pr.at[sidx(k), 0],
            device_id={"expert": partner}, device_id_type=MESH,
        ).wait_send()

    def packed_sent(k, parity):
        for direction in range(2):
            packed_first(k, parity, direction).wait_send()
            packed_second(k, parity, direction).wait_send()
        ref = pin.at[k, 0, pl.ds(0, 2)]
        pltpu.make_async_remote_copy(
            src_ref=ref, dst_ref=ref, send_sem=pps.at[k], recv_sem=pr.at[k, 0],
            device_id={"expert": partner}, device_id_type=MESH,
        ).wait_send()

    ring_sent(None, 0)

    @pl.loop(0, lanes)
    def _(m):
        for parity in range(2):
            ring_sent(2 * m + parity, parity)
            packed_sent(2 * m + parity, parity)

    w_sent()

    @pl.loop(0, NQ)
    def _(q):
        r_all(q).wait_recv()
        total = land[q, 0].astype(F32)
        for i in range(1, ndp):
            total = total + land[q, i].astype(F32)
        grad_ref[:, pl.ds(pl.multiple_of(q * cw, 128), cw)] = total

    @pl.loop(0, NQ)
    def _(q):
        r_all(q).wait_send()


def grad_kernel(mesh, tokens, cotangent, routes_t, gates_t, weight):
    ndp = mesh.shape["dp"]
    ne = mesh.shape["expert"]
    nz = ne // 2
    toks, width = tokens.shape
    cw = width // NQ
    fd = weight.shape[1]
    items = 2 * NQ
    hops = nz // 2 + 1
    nrows = ne * MOST
    dma = pltpu.SemaphoreType.DMA
    anywhere = pl.BlockSpec(memory_space=pl.ANY)
    vmem = pl.BlockSpec(memory_space=pltpu.VMEM)
    return pl.pallas_call(
        functools.partial(kernel, ndp, ne),
        out_shape=jax.ShapeDtypeStruct((fd, width), F32),
        in_specs=[anywhere, anywhere, vmem, vmem, anywhere],
        out_specs=vmem,
        scratch_shapes=[
            pltpu.VMEM((items, ne, toks, cw), BF16),
            pltpu.VMEM((2, ndp, fd, width), BF16),
            pltpu.VMEM((ne, ne, toks), F32),
            pltpu.VMEM((nz, 2 * MOST, 2 * toks), BF16),
            pltpu.VMEM((nz, 2 * MOST, 128), F32),
            pltpu.VMEM((items, nrows, cw), BF16),
            pltpu.VMEM((ndp * fd, nrows), BF16),
            pltpu.VMEM((NQ, ndp, fd, cw), BF16),
            pltpu.VMEM((NQ, ndp, fd, cw), BF16),
            pltpu.VMEM((2, 2, 4 * MOST, toks), BF16),
            pltpu.VMEM((items, 2, 2, 2 * MOST, cw), BF16),
            pltpu.VMEM((items, 2, 3, 2, 2 * MOST, cw), BF16),
            dma((items + 1,)),
            dma((items + 1, 2, hops)),
            dma((items + 1, 2)),
            dma((items + 1, nz)),
            dma((items + 1,)),
            dma((2, ndp, 2)),
            dma,
            dma((NQ,)),
            dma((NQ,)),
            dma((items, 2)),
            dma((items, 2)),
            dma((items,)),
        ],
        compiler_params=pltpu.CompilerParams(
            collective_id=0, has_side_effects=True, vmem_limit_bytes=67043328
        ),
        name="expert_grad",
    )(tokens, cotangent, routes_t, gates_t, weight)


def solution(mesh):
    def per_device(
        tokens, cotangent, routes, slot_gates, gate_up_weight, down_master, first_moment, second_moment
    ):
        grad = grad_kernel(
            mesh, tokens, cotangent, routes.T, slot_gates.T, jnp.swapaxes(gate_up_weight[0], 1, 2)
        )
        master = down_master[0]
        new_first = BETA_ONE * first_moment[0] + (1.0 - BETA_ONE) * grad
        new_second = BETA_TWO * second_moment[0] + (1.0 - BETA_TWO) * grad * grad
        new_down = master - LEARN_RATE * (
            new_first / (jnp.sqrt(new_second) + ADAM_EPS) + DECAY_RATE * master
        )
        return (new_down[None], new_first[None], new_second[None])

    return jax.shard_map(
        per_device,
        mesh=mesh,
        in_specs=(
            P(("dp", "expert"), None),
            P(("dp", "expert"), None),
            P(("dp", "expert"), None),
            P(("dp", "expert"), None),
            P("expert", None, None, "dp"),
            P("expert", "dp", None),
            P("expert", "dp", None),
            P("expert", "dp", None),
        ),
        out_specs=(P("expert", "dp", None), P("expert", "dp", None), P("expert", "dp", None)),
        check_vma=False,
    )
```
